32 devices in a mesh: tm: 2 (over x), cells: 16 (over z, y, core).
Axes of the slice: x: 2, y: 2, z: 4, core: 2. Of those that a mesh axis runs over, the one named last changes fastest.
Arguments:
- filtered: float32 [2, 8192], P('tm', 'cells'), may hold values from -6 to 6
- panels: bfloat16 [2, 8192, 512], P('tm', 'cells'), may hold values from -0.59662135 to 0.59662135
- tiles: bfloat16 [32, 9, 256, 256], P('cells'), may hold values from -0.06666667 to 1.0666667
- neighbours: int32 [32, 9], P('cells'), may hold values from 0 to 31, as said below
- noise_var: float32 [8192], P('cells'), may hold values from 0.5 to 8
- end_smoothed: float32 [8192], P('cells'), may hold values from -6 to 6
Outputs:
- smoothed: float32 [2, 8192], P('tm', 'cells')
The draws below stay inside these ranges and needn't reach their ends.
Inputs may be any that keep to these rules, and one draw needn't show every extreme that they name: `neighbours`: each block row b names 9 distinct block columns, b among them, all within the 10 consecutive blocks, counted cyclically over 32, that begin at block (b // 2 - 2) * 2.
All inputs are finite; a program needn't handle non-finite values.
Results may differ from the reference program's by a relative error of at most 0.00045.
Values may be sent and summed in bfloat16 or wider, within the bound.
A program may use at most 64 MiB of HBM per device.

```python
import math
import jax
import jax.numpy as jnp
from jax import lax

BLK = 256
R = 512
NBR = 9
BLK_DEV = 2
NB = 32
NC = 8192
STEPS = 2


def neighbour_pattern(key):
    pattern_key = jax.random.fold_in(key, 21)
    span_width = 5 * BLK_DEV
    row_numbers = jnp.arange(NB, dtype=jnp.int32)
    slots = jnp.arange(span_width, dtype=jnp.int32)
    scores = jax.random.randint(pattern_key, (NB, span_width), 0, 2 ** 20, dtype=jnp.int32) * span_width + slots[None, :]
    own_slot = 2 * BLK_DEV + row_numbers % BLK_DEV
    scores = jnp.where(slots[None, :] == own_slot[:, None], -1, scores)
    ranked = jnp.argsort(scores, axis=1, stable=True).astype(jnp.int32)
    offsets = ranked[:, :NBR]
    first_block = (row_numbers // BLK_DEV - 2) * BLK_DEV
    return jnp.mod(first_block[:, None] + offsets, NB).astype(jnp.int32)


def draw_neighbours(key, part):
    return neighbour_pattern(key)


def draw_tiles(key, part):
    pattern = neighbour_pattern(key)
    own_tile = (pattern == jnp.arange(NB, dtype=jnp.int32)[:, None]).astype(jnp.float32)
    spread = jax.random.normal(jax.random.fold_in(key, 22), (NB, NBR, BLK, BLK), jnp.float32)
    spread = jnp.clip(spread, -6.0, 6.0) * (0.5 / math.sqrt(NBR * BLK))
    unit_tile = jnp.eye(BLK, dtype=jnp.float32)
    result = spread + own_tile[:, :, None, None] * unit_tile[None, None]
    return result.astype(jnp.bfloat16)


def draw_panels(key, part):
    normalizer = 1.0 / (18.666666 * math.sqrt(R))
    left_ints = jax.random.randint(jax.random.fold_in(key, 1), (NC, R), -7, 8, dtype=jnp.int32).astype(jnp.float32)

    def one_step(step_key):
        right_ints = jax.random.randint(jax.random.fold_in(step_key, 2), (R, R), -7, 8, dtype=jnp.int32).astype(jnp.float32)
        fresh = jax.random.normal(jax.random.fold_in(step_key, 4), (NC, R), jnp.float32)
        mixed = jnp.dot(left_ints, right_ints, precision=lax.Precision.HIGHEST) * normalizer
        unit_value = 0.9 * mixed + 0.3 * fresh
        return jnp.clip(unit_value, -4.0, 4.0)
    step_keys = jax.random.split(jax.random.fold_in(key, 11), STEPS)
    unit_field = lax.map(one_step, step_keys)
    log_ten = math.log(10.0)
    row_draw = jax.random.uniform(jax.random.fold_in(key, 12), (1, NC, 1), jnp.float32)
    column_draw = jax.random.uniform(jax.random.fold_in(key, 13), (STEPS, 1, R), jnp.float32)
    row_scale = 0.3 * jnp.exp(row_draw * log_ten)
    column_scale = 0.2 * jnp.exp(column_draw * log_ten)
    result = 2.25 / math.sqrt(NC) * row_scale * column_scale * unit_field
    return result.astype(jnp.bfloat16)


def block_levels(rng, dims, cuts, least, high):
    loudness = 1.0
    for axis_at, parts in cuts:
        draws = jax.random.uniform(jax.random.fold_in(jax.random.fold_in(rng, 6), axis_at), (parts,), jnp.float32, least / len(cuts), high / len(cuts))
        loudness = loudness * jnp.repeat(jnp.exp(draws), dims[axis_at] // parts).reshape((-1,) + (1,) * (len(dims) - 1 - axis_at))
    return loudness


def noise(rng, dims, scale, bound, cuts=(), kind=jnp.bfloat16):
    loudness = block_levels(rng, dims, cuts, -0.22, 0.18) if cuts else 1.0
    array = jax.random.normal(rng, dims, jnp.float32) * scale * loudness
    return jnp.minimum(jnp.maximum(array, -bound), bound).astype(kind)


def setup_inputs(seed: int = 0) -> dict:
    splits = jax.random.split(jax.random.key(seed), 7)
    return {
        "filtered": noise(splits[0], (STEPS, NC), 1.0, 6.0, ((0, 2), (1, 16)), jnp.float32),
        "panels": draw_panels(jax.random.fold_in(splits[6], 71), 0),
        "tiles": draw_tiles(jax.random.fold_in(splits[6], 71), 0),
        "neighbours": draw_neighbours(jax.random.fold_in(splits[6], 71), 0),
        "noise_var": jnp.clip(jnp.exp(math.log(8.0) - 2.7725887 * jax.random.uniform(splits[4], (NC,), jnp.float32) ** block_levels(splits[4], (NC,), ((0, 16),), -0.2, 0.2)), 0.5, 8.0),
        "end_smoothed": noise(splits[5], (NC,), 1.0, 6.0, ((0, 16),), jnp.float32),
    }


def block_multiply(tiles, neighbours, field):
    block_count = tiles.shape[0]
    blocks = field.reshape(block_count, BLK, -1).astype(jnp.float32)
    total = jnp.zeros(blocks.shape, jnp.float32)
    for column in range(NBR):
        picked = blocks[neighbours[:, column]]
        total = total + jnp.einsum('bij,bjc->bic', tiles[:, column].astype(jnp.float32), picked, precision=lax.Precision.HIGHEST)
    return total.reshape(field.shape)

def cholesky_apply(factor, right_side):
    column = right_side[:, None]
    halfway = lax.linalg.triangular_solve(factor, column, left_side=True, lower=True)
    solved = lax.linalg.triangular_solve(factor, halfway, left_side=True, lower=True, transpose_a=True)
    return solved[:, 0]

def reference(filtered, panels, tiles, neighbours, noise_var, end_smoothed):
    maximal_precision = lax.Precision.HIGHEST

    def backward(subsequent_value, inputs):
        state_mean, panel = inputs
        advected = block_multiply(tiles, neighbours, panel)
        rescaled_rows = advected / noise_var[:, None]
        system = jnp.eye(R, dtype=jnp.float32) + jnp.dot(advected.T, rescaled_rows, precision=maximal_precision)
        factor = jnp.linalg.cholesky(system)
        predicted_state = block_multiply(tiles, neighbours, state_mean.astype(jnp.bfloat16)[:, None])[:, 0]
        rank_projected = jnp.dot(subsequent_value - predicted_state, rescaled_rows, precision=maximal_precision)
        coefficient = cholesky_apply(factor, rank_projected)
        result = state_mean + jnp.dot(panel.astype(jnp.float32), coefficient, precision=maximal_precision)
        return (result, result)
    carried, smoothed = lax.scan(backward, end_smoothed, (filtered, panels), reverse=True)
    return smoothed
```

```python
import functools
import jax
import jax.numpy as jnp
from jax import lax
from jax.experimental import pallas as pl
from jax.experimental.pallas import tpu as pltpu
from jax.sharding import PartitionSpec as P

HI = lax.Precision.HIGHEST
B = 128
MESH = pl.DeviceIdType.MESH


def invert_block(s, n):
    groups = n // 8
    rows = [s[8 * g:8 * g + 8, :] for g in range(groups)]
    lane = lax.broadcasted_iota(jnp.int32, (8, n), 1)
    sub = lax.broadcasted_iota(jnp.int32, (8, n), 0)
    spread = lambda v, j: jnp.broadcast_to(v[j:j + 1, :], (8, n))
    for g in range(groups):
        k = 8 * g
        cols = [[jnp.broadcast_to(rows[i][:, k + j:k + j + 1], (8, n)) for i in range(groups)] for j in range(8)]
        inside = (lane >= k) & (lane < k + 8)
        lead = jnp.where(inside, jnp.where(lane - k == sub, 1.0, 0.0), rows[g])
        d = [cols[j][g] for j in range(8)]
        for j in range(8):
            inverse = 1.0 / spread(d[j], j)
            fresh = spread(lead, j) * inverse
            lead = jnp.where(sub == j, fresh, lead - d[j] * fresh)
            for l in range(j + 1, 8):
                moved = spread(d[l], j) * inverse
                d[l] = jnp.where(sub == j, moved, d[l] - d[j] * moved)
        spreads = [spread(lead, j) for j in range(8)]
        for i in range(groups):
            if i == g:
                continue
            a = jnp.where(inside, 0.0, rows[i])
            b = cols[4][i] * spreads[4]
            for j in range(4):
                a = a - cols[j][i] * spreads[j]
            for j in range(5, 8):
                b = b + cols[j][i] * spreads[j]
            rows[i] = a - b
        rows[g] = lead
    return jnp.concatenate(rows, axis=0)

def inverse_kernel(s_ref, o_ref, w_ref):
    rank = s_ref.shape[-1]
    n = 128
    o_ref[...] = s_ref[...]
    def step(b, _):
        at = pl.multiple_of(b * n, n)
        own = pl.ds(at, n)
        small = invert_block(o_ref[own, own], n)
        w = jnp.dot(small, o_ref[own, :], precision=HI, preferred_element_type=jnp.float32)
        w_ref[...] = w
        w_ref[:, own] = small
        column = o_ref[:, own]
        o_ref[:, own] = jnp.zeros((rank, n), jnp.float32)
        full = jnp.dot(column, w_ref[...], precision=HI, preferred_element_type=jnp.float32)
        o_ref[...] = o_ref[...] - full
        o_ref[own, :] = w_ref[...]
        return 0
    lax.fori_loop(0, rank // n, step, 0)

def inverse(s):
    r = s.shape[-1]
    return pl.pallas_call(inverse_kernel, out_shape=jax.ShapeDtypeStruct((r, r), jnp.float32),
        in_specs=[pl.BlockSpec(memory_space=pltpu.VMEM)], out_specs=pl.BlockSpec(memory_space=pltpu.VMEM),
        scratch_shapes=[pltpu.VMEM((128, r), jnp.float32)],
        compiler_params=pltpu.CompilerParams(vmem_limit_bytes=40 << 20))(s)

def block_pairs(rank):
    count = rank // B
    return [[p for p in range(count // 2) if p % 2 == half] for half in (0, 1)]


def gram_kernel(n, adv_ref, noise_ref, out_ref, scaled, packed, landed, parts, slots, reduced, gathered, other, sems, sems_chip):
    me = lax.axis_index("cells")
    steps, cells, rank = adv_ref.shape
    count = rank // B
    pairs = block_pairs(rank)
    chips = n // 2
    chip, core = me // 2, me % 2
    partner = chip * 2 + (1 - core)
    rows = packed.shape[2] // steps

    barrier = pltpu.get_barrier_semaphore()
    for k in range(1, n):
        pl.semaphore_signal(barrier, inc=1, device_id={"cells": (me + k) % n}, device_id_type=MESH)

    for t in range(steps):
        scaled[...] = adv_ref[t] / noise_ref[...]
        for half in (0, 1):
            for at, p in enumerate(pairs[half]):
                long, short = count - 1 - p, p
                pieces = []
                for r in (long, short):
                    pieces.append(
                        lax.dot_general(
                            scaled[:, r * B : (r + 1) * B],
                            adv_ref[t, :, : (r + 1) * B],
                            (((0,), (0,)), ((), ())),
                            precision=HI,
                            preferred_element_type=jnp.float32,
                        )
                    )
                value = jnp.concatenate(pieces, axis=1)
                per = B * len(pairs[half]) // chips
                for q in range(B // per):
                    packed[half, at * (B // per) + q, t * rows : t * rows + per] = value[q * per : (q + 1) * per]
    pl.semaphore_wait(barrier, n - 1)

    first = pltpu.make_async_remote_copy(
        packed.at[1 - core], landed, sems.at[0], sems.at[1], device_id={"cells": partner}, device_id_type=MESH
    )
    first.start()
    first.wait()
    parts[...] = packed[core] + landed[...]

    def spread(k):
        q = (chip + k) % chips
        return pltpu.make_async_remote_copy(
            parts.at[q], slots.at[k], sems_chip.at[0, k], sems_chip.at[1, k],
            device_id={"cells": q * 2 + core}, device_id_type=MESH,
        )

    def collect(k):
        q = (chip + k) % chips
        return pltpu.make_async_remote_copy(
            reduced, gathered.at[chip], sems_chip.at[2, k], sems_chip.at[3, k],
            device_id={"cells": q * 2 + core}, device_id_type=MESH,
        )

    for k in range(1, chips):
        spread(k).start()
    total = parts[chip]
    for k in range(1, chips):
        spread(k).wait()
        total = total + slots[k]
    reduced[...] = total
    for k in range(1, chips):
        collect(k).start()
    gathered[chip] = total
    for k in range(1, chips):
        collect(k).wait()
    second = pltpu.make_async_remote_copy(
        gathered, other, sems.at[2], sems.at[3], device_id={"cells": partner}, device_id_type=MESH
    )
    second.start()
    second.wait()

    eye = jnp.where(
        lax.broadcasted_iota(jnp.int32, (B, B), 0) == lax.broadcasted_iota(jnp.int32, (B, B), 1), 1.0, 0.0
    )

    def unpack(half, ref):
        each = chips // len(pairs[half])
        for t in range(steps):
            for at, p in enumerate(pairs[half]):
                value = jnp.concatenate(
                    [ref[at * each + q, t * rows : (t + 1) * rows] for q in range(each)], axis=0
                )
                long, short = count - 1 - p, p
                for r, begin in ((long, 0), (short, (long + 1) * B)):
                    for c in range(r + 1):
                        block = value[:, begin + c * B : begin + (c + 1) * B]
                        if c == r:
                            block = block + eye
                        else:
                            out_ref[t, c * B : (c + 1) * B, r * B : (r + 1) * B] = block.T
                        out_ref[t, r * B : (r + 1) * B, c * B : (c + 1) * B] = block

    @pl.when(core == 0)
    def _():
        unpack(0, gathered)
        unpack(1, other)

    @pl.when(core == 1)
    def _():
        unpack(1, gathered)
        unpack(0, other)


def summed_system(advected, noise_var, n):
    steps, cells, rank = advected.shape
    chips = n // 2
    per_half = (rank // B) // 4
    rows = B * per_half // chips * steps
    wide = rank + B
    f32 = jnp.float32
    return pl.pallas_call(
        functools.partial(gram_kernel, n),
        out_shape=jax.ShapeDtypeStruct((steps, rank, rank), f32),
        in_specs=[pl.BlockSpec(memory_space=pltpu.VMEM)] * 2,
        out_specs=pl.BlockSpec(memory_space=pltpu.VMEM),
        scratch_shapes=[
            pltpu.VMEM((cells, rank), f32),
            pltpu.VMEM((2, chips, rows, wide), f32),
            pltpu.VMEM((chips, rows, wide), f32),
            pltpu.VMEM((chips, rows, wide), f32),
            pltpu.VMEM((chips, rows, wide), f32),
            pltpu.VMEM((rows, wide), f32),
            pltpu.VMEM((chips, rows, wide), f32),
            pltpu.VMEM((chips, rows, wide), f32),
            pltpu.SemaphoreType.DMA((4,)),
            pltpu.SemaphoreType.DMA((4, chips)),
        ],
        compiler_params=pltpu.CompilerParams(collective_id=0, has_side_effects=True, vmem_limit_bytes=56 << 20),
    )(advected, noise_var[:, None])


def split3(v):
    a = v.astype(jnp.bfloat16)
    rest = v - a.astype(jnp.float32)
    b = rest.astype(jnp.bfloat16)
    c = (rest - b.astype(jnp.float32)).astype(jnp.bfloat16)
    return a, b, c


def sweep_kernel(n, sections, adv_ref, inv_ref, pan_ref, pred_ref, filt_ref, noise_ref, end_ref, out_ref,
                 later, mine, seen, passed, sem_send, sem_recv, sem_tm):
    me = lax.axis_index("cells")
    section = lax.axis_index("tm")
    steps = adv_ref.shape[0]
    has_next = section < sections - 1
    has_before = section > 0

    barrier = pltpu.get_barrier_semaphore()
    for k in range(1, n):
        pl.semaphore_signal(barrier, inc=1, device_id={"cells": (me + k) % n}, device_id_type=MESH)

    @pl.when(has_next)
    def _():
        pl.semaphore_signal(barrier, inc=1, device_id={"tm": section + 1}, device_id_type=MESH)

    @pl.when(has_before)
    def _():
        pl.semaphore_signal(barrier, inc=1, device_id={"tm": section - 1}, device_id_type=MESH)

    pl.semaphore_wait(barrier, n - 1 + has_next.astype(jnp.int32) + has_before.astype(jnp.int32))

    def handoff():
        return pltpu.make_async_remote_copy(
            later, passed, sem_tm.at[0], sem_tm.at[1], device_id={"tm": section - 1}, device_id_type=MESH
        )

    @pl.when(has_next)
    def _():
        handoff().wait_recv()
        later[...] = passed[...]

    @pl.when(section == sections - 1)
    def _():
        later[...] = end_ref[...]

    for t in reversed(range(steps)):
        gap = (later[...] - pred_ref[t : t + 1]) / noise_ref[...]
        mine[t] = jnp.dot(gap, adv_ref[t], precision=HI, preferred_element_type=jnp.float32)

        def share(k):
            return pltpu.make_async_remote_copy(
                mine.at[t], seen.at[t, me], sem_send.at[t, k], sem_recv.at[t, k],
                device_id={"cells": (me + k) % n}, device_id_type=MESH,
            )

        for k in range(1, n):
            share(k).start()
        seen[t, me] = mine[t]
        for k in range(1, n):
            share(k).wait()
        total = seen[t, 0]
        for k in range(1, n):
            total = total + seen[t, k]
        coefficient = jnp.dot(total, inv_ref[t], precision=HI, preferred_element_type=jnp.float32)
        moved = sum(
            lax.dot_general(c, pan_ref[t], (((1,), (1,)), ((), ())), preferred_element_type=jnp.float32)
            for c in split3(coefficient)
        )
        result = filt_ref[t : t + 1] + moved
        later[...] = result
        out_ref[t : t + 1] = result

    @pl.when(has_before)
    def _():
        handoff().start()
        handoff().wait_send()


def sweep_back(advected, inverses, panels, predicted, filtered, noise_var, end_smoothed, n, sections):
    steps, cells, rank = advected.shape
    f32 = jnp.float32
    return pl.pallas_call(
        functools.partial(sweep_kernel, n, sections),
        out_shape=jax.ShapeDtypeStruct((steps, cells), f32),
        in_specs=[pl.BlockSpec(memory_space=pltpu.VMEM)] * 7,
        out_specs=pl.BlockSpec(memory_space=pltpu.VMEM),
        scratch_shapes=[
            pltpu.VMEM((1, cells), f32),
            pltpu.VMEM((steps, 1, rank), f32),
            pltpu.VMEM((steps, n, 1, rank), f32),
            pltpu.VMEM((1, cells), f32),
            pltpu.SemaphoreType.DMA((steps, n)),
            pltpu.SemaphoreType.DMA((steps, n)),
            pltpu.SemaphoreType.DMA((2,)),
        ],
        compiler_params=pltpu.CompilerParams(collective_id=1, has_side_effects=True, vmem_limit_bytes=40 << 20),
    )(advected, inverses, panels, predicted, filtered, noise_var[None], end_smoothed[None])


def passed_along(value, axis, by):
    size = lax.axis_size(axis)
    return lax.ppermute(value, axis, [(i, (i + by) % size) for i in range(size)])


def per_device(filtered, panels, tiles, neighbours, noise_var, end_smoothed):
    steps_here, cells_here, rank_width = panels.shape
    blocks_here = tiles.shape[0]
    block_cells = tiles.shape[2]
    cell_devices = lax.axis_size("cells")
    time_devices = lax.axis_size("tm")
    block_total = blocks_here * cell_devices
    window_first = (lax.axis_index("cells") - 2) * blocks_here
    position = jnp.mod(neighbours - window_first, block_total)
    rounded_means = filtered.astype(jnp.bfloat16)
    pieces = {0: (panels, rounded_means)}
    for heading in (-1, 1):
        for hops in (1, 2):
            pieces[hops * heading] = passed_along((panels, rounded_means), "cells", -heading * hops)
    window_panels = jnp.concatenate(
        [
            pieces[offset][0].reshape(steps_here, blocks_here, block_cells, rank_width)
            for offset in (-2, -1, 0, 1, 2)
        ],
        axis=1,
    )
    window_means = jnp.concatenate(
        [
            pieces[offset][1].reshape(steps_here, blocks_here, block_cells)
            for offset in (-2, -1, 0, 1, 2)
        ],
        axis=1,
    )
    advected = jnp.einsum(
        "rkij,trkjc->tric", tiles, window_panels[:, position], preferred_element_type=jnp.float32
    ).reshape(steps_here, cells_here, rank_width)
    predicted_state = jnp.einsum(
        "rkij,trkj->tri", tiles, window_means[:, position], preferred_element_type=jnp.float32
    ).reshape(steps_here, cells_here)
    system = summed_system(advected, noise_var, cell_devices)
    inverses = jnp.stack([inverse(system[t]) for t in range(steps_here)])
    return sweep_back(
        advected, inverses, panels, predicted_state, filtered, noise_var, end_smoothed, cell_devices, time_devices
    )


def solution(mesh):
    placed = (
        P("tm", "cells"),
        P("tm", "cells", None),
        P("cells", None, None, None),
        P("cells", None),
        P("cells"),
        P("cells"),
    )
    return jax.shard_map(
        per_device, mesh=mesh, in_specs=placed, out_specs=P("tm", "cells"), check_vma=False
    )
```

```python
import functools
import jax
import jax.numpy as jnp
from jax import lax
from jax.experimental import pallas as pl
from jax.experimental.pallas import tpu as pltpu
from jax.sharding import PartitionSpec as P

HI = lax.Precision.HIGHEST
B = 128
MESH = pl.DeviceIdType.MESH


def invert_block(s, n):
    groups = n // 8
    rows = [s[8 * g:8 * g + 8, :] for g in range(groups)]
    lane = lax.broadcasted_iota(jnp.int32, (8, n), 1)
    sub = lax.broadcasted_iota(jnp.int32, (8, n), 0)
    spread = lambda v, j: jnp.broadcast_to(v[j:j + 1, :], (8, n))
    for g in range(groups):
        k = 8 * g
        cols = [[jnp.broadcast_to(rows[i][:, k + j:k + j + 1], (8, n)) for i in range(groups)] for j in range(8)]
        inside = (lane >= k) & (lane < k + 8)
        lead = jnp.where(inside, jnp.where(lane - k == sub, 1.0, 0.0), rows[g])
        d = [cols[j][g] for j in range(8)]
        for j in range(8):
            inverse = 1.0 / spread(d[j], j)
            fresh = spread(lead, j) * inverse
            lead = jnp.where(sub == j, fresh, lead - d[j] * fresh)
            for l in range(j + 1, 8):
                moved = spread(d[l], j) * inverse
                d[l] = jnp.where(sub == j, moved, d[l] - d[j] * moved)
        spreads = [spread(lead, j) for j in range(8)]
        for i in range(groups):
            if i == g:
                continue
            a = jnp.where(inside, 0.0, rows[i])
            b = cols[4][i] * spreads[4]
            for j in range(4):
                a = a - cols[j][i] * spreads[j]
            for j in range(5, 8):
                b = b + cols[j][i] * spreads[j]
            rows[i] = a - b
        rows[g] = lead
    return jnp.concatenate(rows, axis=0)

def inverse_kernel(s_ref, o_ref, w_ref):
    rank = s_ref.shape[-1]
    n = 128
    o_ref[...] = s_ref[...]
    def step(b, _):
        at = pl.multiple_of(b * n, n)
        own = pl.ds(at, n)
        small = invert_block(o_ref[own, own], n)
        w = jnp.dot(small, o_ref[own, :], precision=HI, preferred_element_type=jnp.float32)
        w_ref[...] = w
        w_ref[:, own] = small
        column = o_ref[:, own]
        o_ref[:, own] = jnp.zeros((rank, n), jnp.float32)
        full = jnp.dot(column, w_ref[...], precision=HI, preferred_element_type=jnp.float32)
        o_ref[...] = o_ref[...] - full
        o_ref[own, :] = w_ref[...]
        return 0
    lax.fori_loop(0, rank // n, step, 0)

def inverse(s):
    r = s.shape[-1]
    return pl.pallas_call(inverse_kernel, out_shape=jax.ShapeDtypeStruct((r, r), jnp.float32),
        in_specs=[pl.BlockSpec(memory_space=pltpu.VMEM)], out_specs=pl.BlockSpec(memory_space=pltpu.VMEM),
        scratch_shapes=[pltpu.VMEM((128, r), jnp.float32)],
        compiler_params=pltpu.CompilerParams(vmem_limit_bytes=40 << 20))(s)

def block_pairs(rank):
    count = rank // B
    return [[p for p in range(count // 2) if p % 2 == half] for half in (0, 1)]


def gram_kernel(n, pan_ref, filt_ref, tiles_ref, near_ref, noise_ref, out_ref, adv_ref, pred_ref,
                window, means, tiles, dense, scaled, packed, landed, parts, slots, reduced, gathered, other,
                sems, sems_chip, sems_halo, sems_mean, sem_tiles):
    me = lax.axis_index("cells")
    steps, cells, rank = adv_ref.shape
    blocks, per_row, size = tiles.shape[:3]
    wide = window.shape[-1]
    chunks = rank // wide
    count = rank // B
    pairs = block_pairs(rank)
    chips = n // 2
    chip, core = me // 2, me % 2
    partner = chip * 2 + (1 - core)
    rows = packed.shape[2] // steps

    fetch = pltpu.make_async_copy(tiles_ref, tiles, sem_tiles)
    fetch.start()
    barrier = pltpu.get_barrier_semaphore()
    for k in range(1, n):
        pl.semaphore_signal(barrier, inc=1, device_id={"cells": (me + k) % n}, device_id_type=MESH)
    pl.semaphore_wait(barrier, n - 1)

    def mean_copy(offset):
        return pltpu.make_async_remote_copy(
            filt_ref, means.at[2 - offset], sems_mean.at[0, 2 - offset], sems_mean.at[1, 2 - offset],
            device_id={"cells": (me + offset + n) % n}, device_id_type=MESH,
        )

    def own_chunk(j):
        return pan_ref.at[:, :, j * wide : (j + 1) * wide]

    def near(j):
        return pltpu.make_async_remote_copy(
            own_chunk(j), window.at[1 + 2 * core, j], sems_halo.at[0, 0, j], sems_halo.at[1, 0, j],
            device_id={"cells": partner}, device_id_type=MESH,
        )

    def far(j, s):
        return pltpu.make_async_remote_copy(
            own_chunk(j), window.at[4 * s, j], sems_halo.at[0, 1 + s, j], sems_halo.at[1, 1 + s, j],
            device_id={"cells": (me + 2 - 4 * s + n) % n}, device_id_type=MESH,
        )

    def forward(j):
        return pltpu.make_async_remote_copy(
            window.at[4 - 4 * core, j], window.at[3 - 2 * core, j],
            sems_halo.at[0, 3, j], sems_halo.at[1, 3, j],
            device_id={"cells": partner}, device_id_type=MESH,
        )

    for offset in (1, -1, 2, -2):
        mean_copy(offset).start()
    for j in range(chunks):
        far(j, 0).start()
        far(j, 1).start()
        near(j).start()

    fetch.wait()
    first_block = (me - 2) * blocks
    total_blocks = n * blocks
    for b in range(blocks):
        places = [(near_ref[b, k] - first_block + total_blocks) % total_blocks for k in range(per_row)]
        for w in range(5 * blocks):
            at = jnp.int32(0)
            found = jnp.int32(0)
            for k in range(per_row):
                hit = (places[k] == w).astype(jnp.int32)
                at = jnp.maximum(at, hit * k)
                found = jnp.maximum(found, hit)
            keep = jnp.full((size, size), found, jnp.int32) > 0
            tile = tiles[b, at].astype(jnp.float32)
            dense[b * size : (b + 1) * size, w * size : (w + 1) * size] = jnp.where(keep, tile, 0.0).astype(jnp.bfloat16)

    for offset in (1, -1, 2, -2):
        mean_copy(offset).wait()
    for t in range(steps):
        total = jnp.zeros((1, cells), jnp.float32)
        for s in range(5):
            row = filt_ref[t : t + 1] if s == 2 else means[s, t : t + 1]
            total = total + lax.dot_general(
                row.astype(jnp.bfloat16), dense[:, s * cells : (s + 1) * cells],
                (((1,), (1,)), ((), ())), preferred_element_type=jnp.float32,
            )
        pred_ref[t : t + 1] = total

    home = {}
    for half in (0, 1):
        for at, p in enumerate(pairs[half]):
            long, short = count - 1 - p, p
            home[long] = (half, at, 0)
            home[short] = (half, at, (long + 1) * B)
    per = rows
    for j in range(chunks):
        here = slice(j * wide, (j + 1) * wide)
        far(j, 1 - core).wait_recv()
        forward(j).start()
        near(j).wait_recv()
        far(j, core).wait_recv()
        forward(j).wait_recv()
        for t in range(steps):
            product = jnp.zeros((cells, wide), jnp.float32)
            for s in range(5):
                piece = pan_ref[t, :, here] if s == 2 else window[s, j, t]
                product = product + jnp.dot(
                    dense[:, s * cells : (s + 1) * cells], piece, preferred_element_type=jnp.float32
                )
            adv_ref[t, :, here] = product
            scaled[t, :, here] = product / noise_ref[...]
            for r in range(j * wide // B, (j + 1) * wide // B):
                value = lax.dot_general(
                    scaled[t, :, r * B : (r + 1) * B],
                    adv_ref[t, :, : (r + 1) * B],
                    (((0,), (0,)), ((), ())),
                    precision=HI,
                    preferred_element_type=jnp.float32,
                )
                half, at, begin = home[r]
                for q in range(B // per):
                    packed[half, at * (B // per) + q, t * rows : (t + 1) * rows, begin : begin + (r + 1) * B] = value[
                        q * per : (q + 1) * per
                    ]
    for j in range(chunks):
        near(j).wait_send()
        far(j, 0).wait_send()
        far(j, 1).wait_send()
        forward(j).wait_send()

    first = pltpu.make_async_remote_copy(
        packed.at[1 - core], landed, sems.at[0], sems.at[1], device_id={"cells": partner}, device_id_type=MESH
    )
    first.start()
    first.wait()
    parts[...] = packed[core] + landed[...]

    def spread(k):
        q = (chip + k) % chips
        return pltpu.make_async_remote_copy(
            parts.at[q], slots.at[k], sems_chip.at[0, k], sems_chip.at[1, k],
            device_id={"cells": q * 2 + core}, device_id_type=MESH,
        )

    def collect(k):
        q = (chip + k) % chips
        return pltpu.make_async_remote_copy(
            reduced, gathered.at[chip], sems_chip.at[2, k], sems_chip.at[3, k],
            device_id={"cells": q * 2 + core}, device_id_type=MESH,
        )

    for k in range(1, chips):
        spread(k).start()
    total = parts[chip]
    for k in range(1, chips):
        spread(k).wait()
        total = total + slots[k]
    reduced[...] = total
    for k in range(1, chips):
        collect(k).start()
    gathered[chip] = total
    for k in range(1, chips):
        collect(k).wait()
    second = pltpu.make_async_remote_copy(
        gathered, other, sems.at[2], sems.at[3], device_id={"cells": partner}, device_id_type=MESH
    )
    second.start()
    second.wait()

    eye = jnp.where(
        lax.broadcasted_iota(jnp.int32, (B, B), 0) == lax.broadcasted_iota(jnp.int32, (B, B), 1), 1.0, 0.0
    )

    def unpack(half, ref):
        each = chips // len(pairs[half])
        for t in range(steps):
            for at, p in enumerate(pairs[half]):
                value = jnp.concatenate(
                    [ref[at * each + q, t * rows : (t + 1) * rows] for q in range(each)], axis=0
                )
                long, short = count - 1 - p, p
                for r, begin in ((long, 0), (short, (long + 1) * B)):
                    for c in range(r + 1):
                        block = value[:, begin + c * B : begin + (c + 1) * B]
                        if c == r:
                            block = block + eye
                        else:
                            out_ref[t, c * B : (c + 1) * B, r * B : (r + 1) * B] = block.T
                        out_ref[t, r * B : (r + 1) * B, c * B : (c + 1) * B] = block

    @pl.when(core == 0)
    def _():
        unpack(0, gathered)
        unpack(1, other)

    @pl.when(core == 1)
    def _():
        unpack(1, gathered)
        unpack(0, other)


def summed_system(panels, filtered, tiles, neighbours, noise_var, n):
    steps, cells, rank = panels.shape
    chips = n // 2
    per_half = (rank // B) // 4
    rows = B * per_half // chips * steps
    wide = rank + B
    chunk = 2 * B
    f32 = jnp.float32
    vmem = pl.BlockSpec(memory_space=pltpu.VMEM)
    return pl.pallas_call(
        functools.partial(gram_kernel, n),
        out_shape=(
            jax.ShapeDtypeStruct((steps, rank, rank), f32),
            jax.ShapeDtypeStruct((steps, cells, rank), f32),
            jax.ShapeDtypeStruct((steps, cells), f32),
        ),
        in_specs=[vmem, vmem, pl.BlockSpec(memory_space=pl.ANY), pl.BlockSpec(memory_space=pltpu.SMEM), vmem],
        out_specs=[vmem] * 3,
        scratch_shapes=[
            pltpu.VMEM((5, rank // chunk, steps, cells, chunk), panels.dtype),
            pltpu.VMEM((5, steps, cells), f32),
            pltpu.VMEM(tiles.shape, tiles.dtype),
            pltpu.VMEM((cells, 5 * cells), tiles.dtype),
            pltpu.VMEM((steps, cells, rank), f32),
            pltpu.VMEM((2, chips, rows, wide), f32),
            pltpu.VMEM((chips, rows, wide), f32),
            pltpu.VMEM((chips, rows, wide), f32),
            pltpu.VMEM((chips, rows, wide), f32),
            pltpu.VMEM((rows, wide), f32),
            pltpu.VMEM((chips, rows, wide), f32),
            pltpu.VMEM((chips, rows, wide), f32),
            pltpu.SemaphoreType.DMA((4,)),
            pltpu.SemaphoreType.DMA((4, chips)),
            pltpu.SemaphoreType.DMA((2, 4, rank // chunk)),
            pltpu.SemaphoreType.DMA((2, 5)),
            pltpu.SemaphoreType.DMA,
        ],
        compiler_params=pltpu.CompilerParams(collective_id=0, has_side_effects=True, vmem_limit_bytes=56 << 20),
    )(panels, filtered, tiles, neighbours, noise_var[:, None])


def split3(v):
    a = v.astype(jnp.bfloat16)
    rest = v - a.astype(jnp.float32)
    b = rest.astype(jnp.bfloat16)
    c = (rest - b.astype(jnp.float32)).astype(jnp.bfloat16)
    return a, b, c


def sweep_kernel(n, sections, adv_ref, inv_ref, pan_ref, pred_ref, filt_ref, noise_ref, end_ref, out_ref,
                 later, mine, seen, passed, sem_send, sem_recv, sem_tm):
    me = lax.axis_index("cells")
    section = lax.axis_index("tm")
    steps = adv_ref.shape[0]
    has_next = section < sections - 1
    has_before = section > 0

    barrier = pltpu.get_barrier_semaphore()
    for k in range(1, n):
        pl.semaphore_signal(barrier, inc=1, device_id={"cells": (me + k) % n}, device_id_type=MESH)

    @pl.when(has_next)
    def _():
        pl.semaphore_signal(barrier, inc=1, device_id={"tm": section + 1}, device_id_type=MESH)

    @pl.when(has_before)
    def _():
        pl.semaphore_signal(barrier, inc=1, device_id={"tm": section - 1}, device_id_type=MESH)

    pl.semaphore_wait(barrier, n - 1 + has_next.astype(jnp.int32) + has_before.astype(jnp.int32))

    def handoff():
        return pltpu.make_async_remote_copy(
            later, passed, sem_tm.at[0], sem_tm.at[1], device_id={"tm": section - 1}, device_id_type=MESH
        )

    @pl.when(has_next)
    def _():
        handoff().wait_recv()
        later[...] = passed[...]

    @pl.when(section == sections - 1)
    def _():
        later[...] = end_ref[...]

    for t in reversed(range(steps)):
        gap = (later[...] - pred_ref[t : t + 1]) / noise_ref[...]
        mine[t] = jnp.dot(gap, adv_ref[t], precision=HI, preferred_element_type=jnp.float32)

        def share(k):
            return pltpu.make_async_remote_copy(
                mine.at[t], seen.at[t, me], sem_send.at[t, k], sem_recv.at[t, k],
                device_id={"cells": (me + k) % n}, device_id_type=MESH,
            )

        for k in range(1, n):
            share(k).start()
        seen[t, me] = mine[t]
        for k in range(1, n):
            share(k).wait()
        total = seen[t, 0]
        for k in range(1, n):
            total = total + seen[t, k]
        coefficient = jnp.dot(total, inv_ref[t], precision=HI, preferred_element_type=jnp.float32)
        moved = sum(
            lax.dot_general(c, pan_ref[t], (((1,), (1,)), ((), ())), preferred_element_type=jnp.float32)
            for c in split3(coefficient)
        )
        result = filt_ref[t : t + 1] + moved
        later[...] = result
        out_ref[t : t + 1] = result

    @pl.when(has_before)
    def _():
        handoff().start()
        handoff().wait_send()


def sweep_back(advected, inverses, panels, predicted, filtered, noise_var, end_smoothed, n, sections):
    steps, cells, rank = advected.shape
    f32 = jnp.float32
    return pl.pallas_call(
        functools.partial(sweep_kernel, n, sections),
        out_shape=jax.ShapeDtypeStruct((steps, cells), f32),
        in_specs=[pl.BlockSpec(memory_space=pltpu.VMEM)] * 7,
        out_specs=pl.BlockSpec(memory_space=pltpu.VMEM),
        scratch_shapes=[
            pltpu.VMEM((1, cells), f32),
            pltpu.VMEM((steps, 1, rank), f32),
            pltpu.VMEM((steps, n, 1, rank), f32),
            pltpu.VMEM((1, cells), f32),
            pltpu.SemaphoreType.DMA((steps, n)),
            pltpu.SemaphoreType.DMA((steps, n)),
            pltpu.SemaphoreType.DMA((2,)),
        ],
        compiler_params=pltpu.CompilerParams(collective_id=1, has_side_effects=True, vmem_limit_bytes=40 << 20),
    )(advected, inverses, panels, predicted, filtered, noise_var[None], end_smoothed[None])


def per_device(filtered, panels, tiles, neighbours, noise_var, end_smoothed):
    cell_devices = lax.axis_size("cells")
    system, advected, predicted = summed_system(panels, filtered, tiles, neighbours, noise_var, cell_devices)
    inverses = jnp.stack([inverse(system[t]) for t in range(panels.shape[0])])
    return sweep_back(
        advected, inverses, panels, predicted, filtered, noise_var, end_smoothed, cell_devices, lax.axis_size("tm")
    )


def solution(mesh):
    placed = (
        P("tm", "cells"),
        P("tm", "cells", None),
        P("cells", None, None, None),
        P("cells", None),
        P("cells"),
        P("cells"),
    )
    return jax.shard_map(
        per_device, mesh=mesh, in_specs=placed, out_specs=P("tm", "cells"), check_vma=False
    )
```

```python
import functools
import jax
import jax.numpy as jnp
from jax import lax
from jax.experimental import pallas as pl
from jax.experimental.pallas import tpu as pltpu
from jax.sharding import PartitionSpec as P

HI = lax.Precision.HIGHEST
B = 128
MESH = pl.DeviceIdType.MESH


def invert_block(s, n):
    groups = n // 8
    rows = [s[8 * g:8 * g + 8, :] for g in range(groups)]
    lane = lax.broadcasted_iota(jnp.int32, (8, n), 1)
    sub = lax.broadcasted_iota(jnp.int32, (8, n), 0)
    spread = lambda v, j: jnp.broadcast_to(v[j:j + 1, :], (8, n))
    for g in range(groups):
        k = 8 * g
        cols = [[jnp.broadcast_to(rows[i][:, k + j:k + j + 1], (8, n)) for i in range(groups)] for j in range(8)]
        inside = (lane >= k) & (lane < k + 8)
        lead = jnp.where(inside, jnp.where(lane - k == sub, 1.0, 0.0), rows[g])
        d = [cols[j][g] for j in range(8)]
        for j in range(8):
            inverse = 1.0 / spread(d[j], j)
            fresh = spread(lead, j) * inverse
            lead = jnp.where(sub == j, fresh, lead - d[j] * fresh)
            for l in range(j + 1, 8):
                moved = spread(d[l], j) * inverse
                d[l] = jnp.where(sub == j, moved, d[l] - d[j] * moved)
        spreads = [spread(lead, j) for j in range(8)]
        for i in range(groups):
            if i == g:
                continue
            a = jnp.where(inside, 0.0, rows[i])
            b = cols[4][i] * spreads[4]
            for j in range(4):
                a = a - cols[j][i] * spreads[j]
            for j in range(5, 8):
                b = b + cols[j][i] * spreads[j]
            rows[i] = a - b
        rows[g] = lead
    return jnp.concatenate(rows, axis=0)

def invert_into(s_ref, o_ref, w_ref):
    rank = s_ref.shape[-1]
    n = 128
    o_ref[...] = s_ref[...]
    def step(b, _):
        at = pl.multiple_of(b * n, n)
        own = pl.ds(at, n)
        small = invert_block(o_ref[own, own], n)
        w = jnp.dot(small, o_ref[own, :], precision=HI, preferred_element_type=jnp.float32)
        w_ref[...] = w
        w_ref[:, own] = small
        column = o_ref[:, own]
        o_ref[:, own] = jnp.zeros((rank, n), jnp.float32)
        full = jnp.dot(column, w_ref[...], precision=HI, preferred_element_type=jnp.float32)
        o_ref[...] = o_ref[...] - full
        o_ref[own, :] = w_ref[...]
        return 0
    lax.fori_loop(0, rank // n, step, 0)


def block_pairs(rank):
    count = rank // B
    return [[p for p in range(count // 2) if p % 2 == half] for half in (0, 1)]


def gram_kernel(n, pan_ref, filt_ref, tiles_ref, near_ref, noise_ref, out_ref, adv_ref, pred_ref,
                window, means, tiles, dense, divisor, scaled, packed, landed, parts, slots, reduced, gathered, other,
                sems, sems_chip, sems_halo, sems_mean, sem_tiles):
    me = lax.axis_index("cells")
    steps, cells, rank = adv_ref.shape
    blocks, per_row, size = tiles.shape[:3]
    wide = window.shape[-1]
    chunks = rank // wide
    count = rank // B
    pairs = block_pairs(rank)
    chips = n // 2
    chip, core = me // 2, me % 2
    partner = chip * 2 + (1 - core)
    rows = packed.shape[2] // steps

    fetch = pltpu.make_async_copy(tiles_ref, tiles, sem_tiles)
    fetch.start()
    barrier = pltpu.get_barrier_semaphore()
    for k in range(1, n):
        pl.semaphore_signal(barrier, inc=1, device_id={"cells": (me + k) % n}, device_id_type=MESH)
    pl.semaphore_wait(barrier, n - 1)

    def mean_copy(offset):
        return pltpu.make_async_remote_copy(
            filt_ref, means.at[2 - offset], sems_mean.at[0, 2 - offset], sems_mean.at[1, 2 - offset],
            device_id={"cells": (me + offset + n) % n}, device_id_type=MESH,
        )

    def own_chunk(j):
        return pan_ref.at[:, :, j * wide : (j + 1) * wide]

    def near(j):
        return pltpu.make_async_remote_copy(
            own_chunk(j), window.at[1 + 2 * core, j], sems_halo.at[0, 0, j], sems_halo.at[1, 0, j],
            device_id={"cells": partner}, device_id_type=MESH,
        )

    def far(j, s):
        return pltpu.make_async_remote_copy(
            own_chunk(j), window.at[4 * s, j], sems_halo.at[0, 1 + s, j], sems_halo.at[1, 1 + s, j],
            device_id={"cells": (me + 2 - 4 * s + n) % n}, device_id_type=MESH,
        )

    def forward(j):
        return pltpu.make_async_remote_copy(
            window.at[4 - 4 * core, j], window.at[3 - 2 * core, j],
            sems_halo.at[0, 3, j], sems_halo.at[1, 3, j],
            device_id={"cells": partner}, device_id_type=MESH,
        )

    for offset in (1, -1, 2, -2):
        mean_copy(offset).start()
    for j in range(chunks):
        far(j, 0).start()
        far(j, 1).start()
        near(j).start()

    divisor[...] = jnp.broadcast_to(noise_ref[...], (B, cells)).T
    fetch.wait()
    first_block = (me - 2) * blocks
    total_blocks = n * blocks
    for b in range(blocks):
        places = [(near_ref[b, k] - first_block + total_blocks) % total_blocks for k in range(per_row)]
        for w in range(5 * blocks):
            at = jnp.int32(0)
            found = jnp.int32(0)
            for k in range(per_row):
                hit = (places[k] == w).astype(jnp.int32)
                at = jnp.maximum(at, hit * k)
                found = jnp.maximum(found, hit)
            keep = jnp.full((size, size), found, jnp.int32) > 0
            tile = tiles[b, at].astype(jnp.float32)
            dense[b * size : (b + 1) * size, w * size : (w + 1) * size] = jnp.where(keep, tile, 0.0).astype(jnp.bfloat16)

    for offset in (1, -1, 2, -2):
        mean_copy(offset).wait()
    for t in range(steps):
        total = jnp.zeros((1, cells), jnp.float32)
        for s in range(5):
            row = filt_ref[t : t + 1] if s == 2 else means[s, t : t + 1]
            total = total + lax.dot_general(
                row.astype(jnp.bfloat16), dense[:, s * cells : (s + 1) * cells],
                (((1,), (1,)), ((), ())), preferred_element_type=jnp.float32,
            )
        pred_ref[t : t + 1] = total

    home = {}
    for half in (0, 1):
        for at, p in enumerate(pairs[half]):
            long, short = count - 1 - p, p
            home[long] = (half, at, 0)
            home[short] = (half, at, (long + 1) * B)
    per = rows
    for j in range(chunks):
        here = slice(j * wide, (j + 1) * wide)
        far(j, 1 - core).wait_recv()
        forward(j).start()
        near(j).wait_recv()
        far(j, core).wait_recv()
        forward(j).wait_recv()
        for t in range(steps):
            product = jnp.zeros((cells, wide), jnp.float32)
            for s in range(5):
                piece = pan_ref[t, :, here] if s == 2 else window[s, j, t]
                product = product + jnp.dot(
                    dense[:, s * cells : (s + 1) * cells], piece, preferred_element_type=jnp.float32
                )
            adv_ref[t, :, here] = product
            scaled[t, :, here] = product / divisor[:, :1]
            for r in range(j * wide // B, (j + 1) * wide // B):
                value = lax.dot_general(
                    scaled[t, :, r * B : (r + 1) * B],
                    adv_ref[t, :, : (r + 1) * B],
                    (((0,), (0,)), ((), ())),
                    precision=HI,
                    preferred_element_type=jnp.float32,
                )
                half, at, begin = home[r]
                for q in range(B // per):
                    packed[half, at * (B // per) + q, t * rows : (t + 1) * rows, begin : begin + (r + 1) * B] = value[
                        q * per : (q + 1) * per
                    ]
    for j in range(chunks):
        near(j).wait_send()
        far(j, 0).wait_send()
        far(j, 1).wait_send()
        forward(j).wait_send()

    first = pltpu.make_async_remote_copy(
        packed.at[1 - core], landed, sems.at[0], sems.at[1], device_id={"cells": partner}, device_id_type=MESH
    )
    first.start()
    first.wait()
    parts[...] = packed[core] + landed[...]

    def spread(k):
        q = (chip + k) % chips
        return pltpu.make_async_remote_copy(
            parts.at[q], slots.at[k], sems_chip.at[0, k], sems_chip.at[1, k],
            device_id={"cells": q * 2 + core}, device_id_type=MESH,
        )

    def collect(k):
        q = (chip + k) % chips
        return pltpu.make_async_remote_copy(
            reduced, gathered.at[chip], sems_chip.at[2, k], sems_chip.at[3, k],
            device_id={"cells": q * 2 + core}, device_id_type=MESH,
        )

    for k in range(1, chips):
        spread(k).start()
    total = parts[chip]
    for k in range(1, chips):
        spread(k).wait()
        total = total + slots[k]
    reduced[...] = total
    for k in range(1, chips):
        collect(k).start()
    gathered[chip] = total

    def across(k, source):
        return pltpu.make_async_remote_copy(
            source, other.at[(chip - k + chips) % chips], sems_chip.at[4, k], sems_chip.at[5, k],
            device_id={"cells": partner}, device_id_type=MESH,
        )

    across(0, reduced).start()
    for k in range(1, chips):
        collect(k).wait_recv()
        across(k, gathered.at[(chip - k + chips) % chips]).start()
    for k in range(1, chips):
        collect(k).wait_send()
    for k in range(chips):
        across(k, reduced).wait()

    eye = jnp.where(
        lax.broadcasted_iota(jnp.int32, (B, B), 0) == lax.broadcasted_iota(jnp.int32, (B, B), 1), 1.0, 0.0
    )

    def unpack(half, ref):
        each = chips // len(pairs[half])
        for t in range(steps):
            for at, p in enumerate(pairs[half]):
                value = jnp.concatenate(
                    [ref[at * each + q, t * rows : (t + 1) * rows] for q in range(each)], axis=0
                )
                long, short = count - 1 - p, p
                for r, begin in ((long, 0), (short, (long + 1) * B)):
                    for c in range(r + 1):
                        block = value[:, begin + c * B : begin + (c + 1) * B]
                        if c == r:
                            block = block + eye
                        else:
                            out_ref[t, c * B : (c + 1) * B, r * B : (r + 1) * B] = block.T
                        out_ref[t, r * B : (r + 1) * B, c * B : (c + 1) * B] = block

    @pl.when(core == 0)
    def _():
        unpack(0, gathered)
        unpack(1, other)

    @pl.when(core == 1)
    def _():
        unpack(1, gathered)
        unpack(0, other)


def summed_system(panels, filtered, tiles, neighbours, noise_var, n):
    steps, cells, rank = panels.shape
    chips = n // 2
    per_half = (rank // B) // 4
    rows = B * per_half // chips * steps
    wide = rank + B
    chunk = 2 * B
    f32 = jnp.float32
    vmem = pl.BlockSpec(memory_space=pltpu.VMEM)
    return pl.pallas_call(
        functools.partial(gram_kernel, n),
        out_shape=(
            jax.ShapeDtypeStruct((steps, rank, rank), f32),
            jax.ShapeDtypeStruct((steps, cells, rank), f32),
            jax.ShapeDtypeStruct((steps, cells), f32),
        ),
        in_specs=[vmem, vmem, pl.BlockSpec(memory_space=pl.ANY), pl.BlockSpec(memory_space=pltpu.SMEM), vmem],
        out_specs=[vmem] * 3,
        scratch_shapes=[
            pltpu.VMEM((5, rank // chunk, steps, cells, chunk), panels.dtype),
            pltpu.VMEM((5, steps, cells), f32),
            pltpu.VMEM(tiles.shape, tiles.dtype),
            pltpu.VMEM((cells, 5 * cells), tiles.dtype),
            pltpu.VMEM((cells, B), f32),
            pltpu.VMEM((steps, cells, rank), f32),
            pltpu.VMEM((2, chips, rows, wide), f32),
            pltpu.VMEM((chips, rows, wide), f32),
            pltpu.VMEM((chips, rows, wide), f32),
            pltpu.VMEM((chips, rows, wide), f32),
            pltpu.VMEM((rows, wide), f32),
            pltpu.VMEM((chips, rows, wide), f32),
            pltpu.VMEM((chips, rows, wide), f32),
            pltpu.SemaphoreType.DMA((2,)),
            pltpu.SemaphoreType.DMA((6, chips)),
            pltpu.SemaphoreType.DMA((2, 4, rank // chunk)),
            pltpu.SemaphoreType.DMA((2, 5)),
            pltpu.SemaphoreType.DMA,
        ],
        compiler_params=pltpu.CompilerParams(collective_id=0, has_side_effects=True, vmem_limit_bytes=56 << 20),
    )(panels, filtered, tiles, neighbours, noise_var[None])


def split3(v):
    a = v.astype(jnp.bfloat16)
    rest = v - a.astype(jnp.float32)
    b = rest.astype(jnp.bfloat16)
    c = (rest - b.astype(jnp.float32)).astype(jnp.bfloat16)
    return a, b, c


def sweep_kernel(n, sections, adv_ref, system_ref, pan_ref, pred_ref, filt_ref, noise_ref, end_ref, out_ref,
                 inv_ref, strip, later, mine, seen, passed, sem_send, sem_recv, sem_tm):
    me = lax.axis_index("cells")
    section = lax.axis_index("tm")
    steps = adv_ref.shape[0]
    has_next = section < sections - 1
    has_before = section > 0

    barrier = pltpu.get_barrier_semaphore()
    for k in range(1, n):
        pl.semaphore_signal(barrier, inc=1, device_id={"cells": (me + k) % n}, device_id_type=MESH)

    @pl.when(has_next)
    def _():
        pl.semaphore_signal(barrier, inc=1, device_id={"tm": section + 1}, device_id_type=MESH)

    @pl.when(has_before)
    def _():
        pl.semaphore_signal(barrier, inc=1, device_id={"tm": section - 1}, device_id_type=MESH)

    for t in range(steps):
        invert_into(system_ref.at[t], inv_ref.at[t], strip)

    pl.semaphore_wait(barrier, n - 1 + has_next.astype(jnp.int32) + has_before.astype(jnp.int32))

    def handoff():
        return pltpu.make_async_remote_copy(
            later, passed, sem_tm.at[0], sem_tm.at[1], device_id={"tm": section - 1}, device_id_type=MESH
        )

    @pl.when(has_next)
    def _():
        handoff().wait_recv()
        later[...] = passed[...]

    @pl.when(section == sections - 1)
    def _():
        later[...] = end_ref[...]

    for t in reversed(range(steps)):
        gap = (later[...] - pred_ref[t : t + 1]) / noise_ref[...]
        mine[t] = jnp.dot(gap, adv_ref[t], precision=HI, preferred_element_type=jnp.float32)

        def share(k):
            return pltpu.make_async_remote_copy(
                mine.at[t], seen.at[t, me], sem_send.at[t, k], sem_recv.at[t, k],
                device_id={"cells": (me + k) % n}, device_id_type=MESH,
            )

        for k in range(1, n):
            share(k).start()
        seen[t, me] = mine[t]
        for k in range(1, n):
            share(k).wait()
        total = seen[t, 0]
        for k in range(1, n):
            total = total + seen[t, k]
        coefficient = jnp.dot(total, inv_ref[t], precision=HI, preferred_element_type=jnp.float32)
        moved = sum(
            lax.dot_general(c, pan_ref[t], (((1,), (1,)), ((), ())), preferred_element_type=jnp.float32)
            for c in split3(coefficient)
        )
        result = filt_ref[t : t + 1] + moved
        later[...] = result
        out_ref[t : t + 1] = result

    @pl.when(has_before)
    def _():
        handoff().start()
        handoff().wait_send()


def sweep_back(advected, system, panels, predicted, filtered, noise_var, end_smoothed, n, sections):
    steps, cells, rank = advected.shape
    f32 = jnp.float32
    return pl.pallas_call(
        functools.partial(sweep_kernel, n, sections),
        out_shape=jax.ShapeDtypeStruct((steps, cells), f32),
        in_specs=[pl.BlockSpec(memory_space=pltpu.VMEM)] * 7,
        out_specs=pl.BlockSpec(memory_space=pltpu.VMEM),
        scratch_shapes=[
            pltpu.VMEM((steps, rank, rank), f32),
            pltpu.VMEM((B, rank), f32),
            pltpu.VMEM((1, cells), f32),
            pltpu.VMEM((steps, 1, rank), f32),
            pltpu.VMEM((steps, n, 1, rank), f32),
            pltpu.VMEM((1, cells), f32),
            pltpu.SemaphoreType.DMA((steps, n)),
            pltpu.SemaphoreType.DMA((steps, n)),
            pltpu.SemaphoreType.DMA((2,)),
        ],
        compiler_params=pltpu.CompilerParams(collective_id=1, has_side_effects=True, vmem_limit_bytes=40 << 20),
    )(advected, system, panels, predicted, filtered, noise_var[None], end_smoothed[None])


def per_device(filtered, panels, tiles, neighbours, noise_var, end_smoothed):
    cell_devices = lax.axis_size("cells")
    system, advected, predicted = summed_system(panels, filtered, tiles, neighbours, noise_var, cell_devices)
    return sweep_back(
        advected, system, panels, predicted, filtered, noise_var, end_smoothed, cell_devices, lax.axis_size("tm")
    )


def solution(mesh):
    placed = (
        P("tm", "cells"),
        P("tm", "cells", None),
        P("cells", None, None, None),
        P("cells", None),
        P("cells"),
        P("cells"),
    )
    return jax.shard_map(
        per_device, mesh=mesh, in_specs=placed, out_specs=P("tm", "cells"), check_vma=False
    )
```
